32 devices in a mesh: pipe: 4 (over x, core), expert: 8 (over z, y).
Axes of the slice: x: 2, y: 2, z: 4, core: 2. Of those that a mesh axis runs over, the one named last changes fastest.
Arguments:
- tokens: bfloat16 [1024, 6144], P('expert'), may hold values from -6 to 6
- expert_ids: int32 [1024, 2], P('expert'), may hold values from 0 to 7, as said below
- gate_weight: bfloat16 [6144, 16384], P(None, 'expert'), may hold values from -0.078125 to 0.078125
- up_weight: bfloat16 [6144, 16384], P(None, 'expert'), may hold values from -0.078125 to 0.078125
- d_hidden: bfloat16 [256, 16384], P('pipe', 'expert'), may hold values from -6 to 6
Outputs:
- hidden: bfloat16 [256, 16384], P('pipe', 'expert')
- d_tokens: float32 [1024, 6144], P('expert', 'pipe')
The draws below stay inside these ranges and needn't reach their ends.
Inputs may be any that keep to these rules, and one draw needn't show every extreme that they name: `expert_ids`: the two ids of a token differ. Among the 128 tokens of one block at least 8 and at most 32 name expert 0, and in every draw some block has exactly 32 such tokens.
All inputs are finite; a program needn't handle non-finite values.
Results may differ from the reference program's by a relative error of at most 0.0029.
Values may be sent and summed in bfloat16 or wider, within the bound.
A program may use at most 128 MiB of HBM per device.

```python
import jax
import jax.numpy as jnp
from jax import lax

D = 6144
FF = 16384
EXPERTS = 8
TOPK = 2
TOK_DEV = 128
CAP = 32
SPAN = 8
TOKENS = 1024
ROWS = 256
N_PIPE = 4
N_EXPERT = 8


def draw_expert_ids(key, part):
    blocks = TOKENS // TOK_DEV
    key_list = jax.random.split(jax.random.fold_in(key, 17), 6)
    counts = jax.random.randint(key_list[0], (blocks,), CAP // 4, CAP + 1)
    full_block = jax.random.randint(key_list[1], (), 0, blocks)
    counts = jnp.where(jnp.arange(blocks) == full_block, CAP, counts)
    scores = jax.random.randint(key_list[2], (blocks, TOK_DEV), 0, 1 << 20) * TOK_DEV + jnp.arange(TOK_DEV)
    token_rank = jnp.argsort(jnp.argsort(scores, axis=1), axis=1)
    chosen = token_rank < counts[:, None]
    lead_id = jax.random.randint(key_list[3], (blocks, TOK_DEV), 1, EXPERTS)
    offset = jax.random.randint(key_list[4], (blocks, TOK_DEV), 1, EXPERTS - 1)
    second = 1 + (lead_id - 1 + offset) % (EXPERTS - 1)
    lead_id = jnp.where(chosen, 0, lead_id)
    swapped = jax.random.randint(key_list[5], (blocks, TOK_DEV), 0, 2) == 1
    column_one = jnp.where(swapped, second, lead_id)
    column_two = jnp.where(swapped, lead_id, second)
    return jnp.stack([column_one, column_two], axis=2).reshape(TOKENS, TOPK).astype(jnp.int32)


def steps_of(key, shape, pieces, smallest, largest):
    loudness, own = 1.0, jax.random.fold_in(key, 6)
    for position, shards_of in pieces:
        steps = jnp.exp(jax.random.uniform(jax.random.fold_in(own, position), (shards_of,), jnp.float32, smallest / len(pieces), largest / len(pieces)))
        loudness = loudness * jnp.repeat(steps, shape[position] // shards_of).reshape([-1 if axis == position else 1 for axis in range(len(shape))])
    return loudness


def bell_draw(key, extent, spread, bound, pieces=(), kind=jnp.bfloat16):
    values = spread * jax.random.normal(key, extent, jnp.float32)
    if pieces:
        values = values * steps_of(key, extent, pieces, -0.22, 0.18)
    return jnp.clip(values, -bound, bound).astype(kind)


def setup_inputs(seed: int = 0) -> dict:
    key_of = jax.random.split(jax.random.key(seed), 6)
    return {
        "tokens": bell_draw(key_of[0], (TOKENS, D), 1.0, 6.0, ((0, 8),)),
        "expert_ids": draw_expert_ids(jax.random.fold_in(key_of[5], 71), 0),
        "gate_weight": bell_draw(key_of[2], (D, FF), D ** -0.5, 0.078125, ((1, 8),)),
        "up_weight": bell_draw(key_of[3], (D, FF), D ** -0.5, 0.078125, ((1, 8),)),
        "d_hidden": bell_draw(key_of[4], (ROWS, FF), 1.0, 6.0, ((0, 4), (1, 8))),
    }


def reference(tokens, expert_ids, gate_weight, up_weight, d_hidden):
    blocks = N_EXPERT
    is_named = jnp.any(expert_ids == 0, axis=1).astype(jnp.int32).reshape(blocks, TOK_DEV)
    slot_before = jnp.cumsum(is_named, axis=1) - is_named
    positions = jnp.arange(CAP, dtype=jnp.int32)
    select = ((is_named[:, :, None] == 1) & (slot_before[:, :, None] == positions)).astype(jnp.float32)
    inputs = tokens.reshape(blocks, TOK_DEV, D).astype(jnp.float32)
    routed = jnp.einsum("etc,etd->ecd", select, inputs, precision=lax.Precision.HIGHEST).astype(jnp.bfloat16)
    routed = routed.reshape(blocks, N_PIPE, SPAN, D).transpose(1, 0, 2, 3).reshape(N_PIPE, blocks * SPAN, D)
    upstream_all = d_hidden.reshape(N_PIPE, blocks * SPAN, FF)

    def one_group(index):
        rows_in = lax.dynamic_index_in_dim(routed, index, 0, keepdims=False)
        upstream = lax.dynamic_index_in_dim(upstream_all, index, 0, keepdims=False).astype(jnp.float32)
        gate_value = jnp.dot(rows_in, gate_weight, preferred_element_type=jnp.float32)
        up_value = jnp.dot(rows_in, up_weight, preferred_element_type=jnp.float32)
        sigmoid_gate = jax.nn.sigmoid(gate_value)
        activated = gate_value * sigmoid_gate
        hidden_part = (activated * up_value).astype(jnp.bfloat16)
        d_gate = (upstream * up_value * sigmoid_gate * (1.0 + gate_value * (1.0 - sigmoid_gate))).astype(jnp.bfloat16)
        d_up = (upstream * activated).astype(jnp.bfloat16)
        d_rows = jnp.dot(d_gate, gate_weight.T, preferred_element_type=jnp.float32)
        d_rows = d_rows + jnp.dot(d_up, up_weight.T, preferred_element_type=jnp.float32)
        return hidden_part, d_rows

    hidden, d_parts = lax.map(one_group, jnp.arange(N_PIPE, dtype=jnp.int32))
    d_slots = d_parts.reshape(N_PIPE, blocks, SPAN, D).transpose(1, 0, 2, 3).reshape(blocks, CAP, D)
    d_tokens = jnp.einsum("etc,ecd->etd", select, d_slots, precision=lax.Precision.HIGHEST)
    return hidden.reshape(ROWS, FF), d_tokens.reshape(TOKENS, D)
```

```python
import functools
import math

import jax
import jax.numpy as jnp
from jax import lax
from jax.experimental import pallas as pl
from jax.experimental.pallas import tpu as pltpu
from jax.sharding import PartitionSpec as P

CAP = 32
CORES = 2
UNIT = 16
STEPS = 6
MESH_ID = pl.DeviceIdType.MESH
scope = jax.named_scope


def slot_select(expert_ids, first_slot, slot_count):
    is_named = jnp.any(expert_ids == 0, axis=1).astype(jnp.int32)
    slot_before = jnp.cumsum(is_named) - is_named
    positions = first_slot + jnp.arange(slot_count, dtype=jnp.int32)
    marked = (is_named[:, None] == 1) & (slot_before[:, None] == positions[None, :])
    return marked.astype(jnp.float32)


def plain_body(tokens, expert_ids, gate_weight, up_weight, d_hidden):
    hidden_units = gate_weight.shape[1]
    slot_span = CAP // lax.axis_size("pipe")
    own_select = slot_select(expert_ids, lax.axis_index("pipe") * slot_span, slot_span)
    routed = jnp.einsum(
        "tj,td->jd", own_select.astype(jnp.bfloat16), tokens, preferred_element_type=jnp.float32
    ).astype(jnp.bfloat16)
    piece = lax.all_gather(routed, "expert", axis=0, tiled=True)
    gate_part = jnp.dot(piece, gate_weight, preferred_element_type=jnp.float32)
    up_part = jnp.dot(piece, up_weight, preferred_element_type=jnp.float32)
    joined = jnp.concatenate([gate_part, up_part], axis=1)
    gate_value = joined[:, :hidden_units]
    up_value = joined[:, hidden_units:]
    sigmoid_gate = jax.nn.sigmoid(gate_value)
    activated = gate_value * sigmoid_gate
    hidden = (activated * up_value).astype(jnp.bfloat16)
    upstream = d_hidden.astype(jnp.float32)
    d_gate = (
        upstream * up_value * sigmoid_gate * (1.0 + gate_value * (1.0 - sigmoid_gate))
    ).astype(jnp.bfloat16)
    d_up = (upstream * activated).astype(jnp.bfloat16)
    result = jnp.einsum("nh,dh->nd", d_gate, gate_weight, preferred_element_type=jnp.float32)
    slot_grads = lax.psum_scatter(
        result + jnp.einsum("nh,dh->nd", d_up, up_weight, preferred_element_type=jnp.float32),
        "expert",
        scatter_dimension=0,
        tiled=True,
    )
    pieces = lax.all_to_all(slot_grads, "pipe", split_axis=1, concat_axis=0, tiled=True)
    full_select = slot_select(expert_ids, 0, CAP)
    d_tokens = jnp.einsum("tc,cd->td", full_select, pieces, precision=lax.Precision.HIGHEST)
    return (hidden, d_tokens)


def named_counts(ids, count):
    row_id = lax.broadcasted_iota(jnp.int32, (count, count), 0)
    col_id = lax.broadcasted_iota(jnp.int32, (count, count), 1)
    named_row = jnp.where((ids[0:1, :] == 0) | (ids[1:2, :] == 0), 1.0, 0.0)
    across = jnp.broadcast_to(named_row, (count, count))
    named_col = jnp.sum(jnp.where(row_id == col_id, across, 0.0), axis=1, keepdims=True)
    before_col = jnp.sum(jnp.where(col_id < row_id, across, 0.0), axis=1, keepdims=True)
    down = jnp.broadcast_to(named_col, (count, count))
    before_row = jnp.sum(jnp.where(row_id < col_id, down, 0.0), axis=0, keepdims=True)
    return named_row, before_row, named_col, before_col


def place_kernel(placed, slots, hid_in, dtok, hid_out, rows_out, copy_sem):
    groups, unit, features = slots.shape
    tile = rows_out.shape[2]
    hid_copy = pltpu.make_async_copy(hid_in, hid_out, copy_sem.at[0])
    hid_copy.start()
    copies = [hid_copy]
    for n in range(features // tile):
        cols = slice(n * tile, (n + 1) * tile)
        rows_out[n] = jnp.dot(
            placed[...], slots[:, :, cols].reshape(groups * unit, tile),
            precision=lax.Precision.HIGHEST, preferred_element_type=jnp.float32)
        copy = pltpu.make_async_copy(rows_out.at[n], dtok.at[:, cols], copy_sem.at[n + 1])
        copy.start()
        copies.append(copy)
    for copy in copies:
        copy.wait()


def flip(value, bit):
    return value + bit - 2 * bit * lax.rem(value // bit, 2)


def expert_kernel(nz, ny, tok, ids, gate, up, dh, hid, slots, placed,
                  tokv, own, oth, w, wt, acc, dhv, dgv, duv, hst,
                  csend, crecv, full, keep, ysend, yrecv, zsend, zrecv, fin, xsend,
                  zsend_f, zrecv_f, keep_f, ysend_f, yrecv_f,
                  load_sem, send_sem, recv_sem):
    pipe, expert = lax.axis_index("pipe"), lax.axis_index("expert")
    x, c = pipe // CORES, lax.rem(pipe, CORES)
    z, y = expert // ny, lax.rem(expert, ny)
    half_steps = STEPS // 2
    lead = half_steps
    width = tokv.shape[2]
    half = w.shape[4]
    count = tok.shape[0]
    blocks = nz * ny
    span = width * half_steps
    ring = range(1, nz)
    z_pair = {}
    for d in ring:
        other_z = z
        for k in range(nz.bit_length() - 1):
            if d >> k & 1:
                other_z = flip(other_z, 1 << k)
        z_pair[d] = other_z
    core_peer = (x * CORES + 1 - c, expert)
    x_peer = ((1 - x) * CORES + c, expert)
    y_peer = (pipe, z * ny + 1 - y)
    z_peer = {d: (pipe, z_pair[d] * ny + y) for d in ring}

    marks = {"load": {}, "recv": {}}
    sent_bytes = [0]

    def mark(kind, key):
        return marks[kind].setdefault(key, len(marks[kind]))

    def load(key, src, dst):
        pltpu.make_async_copy(src, dst, load_sem.at[mark("load", key)]).start()

    def loaded(key, ref):
        pltpu.make_async_copy(ref, ref, load_sem.at[marks["load"][key]]).wait()

    def send(key, src, dst, device):
        pltpu.make_async_remote_copy(
            src_ref=src, dst_ref=dst, send_sem=send_sem.at[0], recv_sem=recv_sem.at[mark("recv", key)],
            device_id=device, device_id_type=MESH_ID).start()
        sent_bytes[0] += math.prod(src.shape) * src.dtype.itemsize

    def landed(key, ref):
        with scope("_".join(str(k) for k in key)):
            pltpu.make_async_copy(ref, ref, recv_sem.at[marks["recv"][key]]).wait()

    def offset(other, s):
        part = c if other == 0 else 1 - c
        where = 1 - x if s < half_steps else x
        return pl.multiple_of((where * CORES + part) * span + (s % half_steps) * width, 128)

    barrier = pltpu.get_barrier_semaphore()
    peers = [core_peer, x_peer, y_peer] + [z_peer[d] for d in ring]
    for peer in peers:
        pl.semaphore_signal(barrier, inc=1, device_id=peer, device_id_type=MESH_ID)

    mine = pl.ds(pl.multiple_of(c * half, 128), half)
    others = pl.ds(pl.multiple_of((1 - c) * half, 128), half)
    for s in range(STEPS):
        load(("tok", s), tok.at[:, pl.ds(offset(0, s), width)], tokv.at[s])

    named_row, before_row, named_col, before_col = named_counts(ids, count)
    slot_id = (lax.broadcasted_iota(jnp.int32, (UNIT, count), 0) + x * UNIT).astype(jnp.float32)
    select = jnp.where((before_row == slot_id) & (named_row == 1.0), 1.0, 0.0).astype(jnp.bfloat16)

    def load_weights(s):
        for other in (0, 1):
            rows = pl.ds(offset(other, s), width)
            load(("w", s), gate.at[rows, mine], w.at[s, other, 0])
            load(("w", s), up.at[rows, mine], w.at[s, other, 1])

    weight_order = [0, lead] + [s for s in range(STEPS) if s not in (0, lead)]
    for s in weight_order[:2]:
        load_weights(s)
    with scope("barrier"):
        pl.semaphore_wait(barrier, len(peers))

    for s in range(STEPS):
        loaded(("tok", s), tokv.at[s])
        own[s, expert] = jnp.dot(
            select, tokv[s], preferred_element_type=jnp.float32).astype(jnp.bfloat16)
        for d in ring:
            send(("zin", s), own.at[s, expert], own.at[s, expert], z_peer[d])
        send(("yin", s), own.at[s, expert], own.at[s, expert], y_peer)
        if s + 2 < STEPS:
            load_weights(weight_order[s + 2])
    load(("dh",), dh.at[:, mine], dhv.at[c])
    send(("dhin",), dh.at[:, others], dhv.at[c], core_peer)
    lane = lax.broadcasted_iota(jnp.int32, (count, CORES * UNIT), 1).astype(jnp.float32)
    placed[...] = jnp.where((before_col == lane) & (named_col == 1.0), 1.0, 0.0)

    waited, turned = set(), set()

    def weights_in(s):
        if s not in waited:
            waited.add(s)
            with scope(f"w{s}"):
                loaded(("w", s), w.at[s])

    def turn(other, s, mats=(0, 1)):
        weights_in(s)
        turned.add((other, s))
        with scope(f"turn{other}{s}"):
            for m in mats:
                wt[s, other, m] = w[s, other, m].T

    def relay(s):
        landed(("zin", s), own.at[s, pl.ds(0, nz - 1)])
        for d in ring:
            place = z_pair[d] * ny + y
            send(("yin", s), own.at[s, place], own.at[s, place], y_peer)

    def share(s):
        landed(("yin", s), own.at[s, pl.ds(0, nz)])
        send(("cin", s), own.at[s], oth.at[s], core_peer)

    started = []

    def forward(other, s, also=()):
        weights_in(s)
        if other == 1:
            landed(("cin", s), oth.at[s])
        for _, t in also:
            weights_in(t)
        turned.update(also)
        with scope(f"fwd{other}{s}"):
            block = (own if other == 0 else oth)[s].reshape(blocks * UNIT, width)
            for m in (0, 1):
                for o, t in also:
                    wt[t, o, m] = w[t, o, m].T
                term = jnp.dot(block, w[s, other, m], preferred_element_type=jnp.float32)
                if started:
                    acc[m] += term
                else:
                    acc[m] = term
            started.append(s)

    turn(0, 0)
    turn(1, 0)
    turn(0, 3)
    turn(1, 3, [0])
    relay(0)
    turn(1, 3, [1])
    relay(1)
    turn(1, 1, [0])
    relay(2)
    share(0)
    turn(1, 1, [1])
    relay(3)
    share(1)
    forward(0, 0, [(0, 1)])
    relay(4)
    share(2)
    forward(1, 0, [(1, 2)])
    relay(5)
    share(3)
    forward(0, 1, [(1, 4)])
    forward(1, 1, [(0, 2)])
    share(4)
    forward(0, 2, [(1, 5)])
    forward(1, 2, [(0, 4)])
    forward(0, 3)
    share(5)
    forward(1, 3)
    forward(0, 4, [(0, 5)])
    forward(1, 4)
    forward(0, 5)
    forward(1, 5)

    loaded(("dh",), dhv.at[0])
    landed(("dhin",), dhv.at[0])
    tile = 256 if half % 256 == 0 else half
    with scope("epilogue"):
        for n in range(0, half, tile):
            cols = slice(n, n + tile)
            gate_value, up_value = acc[0, :, cols], acc[1, :, cols]
            first = dhv[0, :, cols].astype(jnp.float32).reshape(blocks, UNIT // 2, tile)
            second = dhv[1, :, cols].astype(jnp.float32).reshape(blocks, UNIT // 2, tile)
            upstream = jnp.stack([first, second], axis=1).reshape(blocks * UNIT, tile)
            sigmoid_gate = jax.nn.sigmoid(gate_value)
            activated = gate_value * sigmoid_gate
            hidden = (activated * up_value).reshape(blocks, 2, UNIT // 2, tile)
            for q in (0, 1):
                hst[q, :, cols] = hidden[:, q].reshape(blocks * UNIT // 2, tile).astype(jnp.bfloat16)
            dgv[:, cols] = (
                upstream * up_value * sigmoid_gate * (1.0 + gate_value * (1.0 - sigmoid_gate))
            ).astype(jnp.bfloat16)
            duv[:, cols] = (upstream * activated).astype(jnp.bfloat16)
    load(("hid",), hst.at[c], hid.at[:, mine])

    def backward(other, s):
        if (other, s) in turned:
            return jnp.dot(
                dgv[...], wt[s, other, 0], preferred_element_type=jnp.float32
            ) + jnp.dot(duv[...], wt[s, other, 1], preferred_element_type=jnp.float32)
        contract = (((1,), (1,)), ((), ()))
        return lax.dot_general(
            dgv[...], w[s, other, 0], contract, preferred_element_type=jnp.float32
        ) + lax.dot_general(duv[...], w[s, other, 1], contract, preferred_element_type=jnp.float32)

    turn_of = {}

    def back_other(s):
        turn_of[s] = len(turn_of) % 2
        with scope(f"bwd1{s}"):
            csend[s] = backward(1, s).astype(jnp.bfloat16)
        send(("csum", s), csend.at[s], crecv.at[s], core_peer)

    def back_own(s):
        with scope(f"bwd0{s}"):
            full[turn_of[s]] = backward(0, s).reshape(blocks, UNIT, width)

    def core_add(s):
        landed(("csum", s), crecv.at[s])
        with scope(f"cadd{s}"):
            side = turn_of[s]
            full[side] = full[side] + crecv[s].astype(jnp.float32).reshape(blocks, UNIT, width)
            if s == lead:
                for d in ring:
                    zsend_f[d - 1] = full[side, pl.ds(z_pair[d] * ny, ny)].astype(jnp.bfloat16)
                    send(("zsum", s), zsend_f.at[d - 1], zrecv_f.at[d - 1], z_peer[d])
                keep_f[...] = full[side, pl.ds(z * ny, ny)]
            else:
                for d in [*ring, 0]:
                    place = (z_pair[d] if d else z) * ny
                    ysend[s, d] = full[side, place + 1 - y].astype(jnp.bfloat16)
                    send(("ysum", s, d), ysend.at[s, d], yrecv.at[s, d], y_peer)
                for d in [*ring, 0]:
                    keep[s, d] = full[side, (z_pair[d] if d else z) * ny + y]

    def lead_add():
        landed(("zsum", lead), zrecv_f)
        total = keep_f[...]
        for d in ring:
            total = total + zrecv_f[d - 1].astype(jnp.float32)
        keep_f[...] = total
        ysend_f[...] = keep_f[1 - y].astype(jnp.bfloat16)
        send(("ysum", lead), ysend_f, yrecv_f, y_peer)

    def y_add(s):
        for d in ring:
            landed(("ysum", s, d), yrecv.at[s, d])
            zsend[s, d - 1] = (keep[s, d] + yrecv[s, d].astype(jnp.float32)).astype(jnp.bfloat16)
            send(("zsum", s), zsend.at[s, d - 1], zrecv.at[s, d - 1], z_peer[d])

    def finish(s):
        if s == lead:
            landed(("ysum", s), yrecv_f)
            done = keep_f[y] + yrecv_f[...].astype(jnp.float32)
        else:
            landed(("ysum", s, 0), yrecv.at[s, 0])
            fin[s] = keep[s, 0] + yrecv[s, 0].astype(jnp.float32)
            landed(("zsum", s), zrecv.at[s])
            done = fin[s]
            for d in ring:
                done = done + zrecv[s, d - 1].astype(jnp.float32)
        cols = slice((s % half_steps) * width, (s % half_steps + 1) * width)
        if s < half_steps:
            xsend[s] = done
            send(("xsum",), xsend.at[s], slots.at[x, :, cols], x_peer)
        else:
            slots[x, :, cols] = done

    back_other(0)
    back_own(0)
    back_other(3)
    core_add(0)
    send(("hidin",), hst.at[1 - c], hid.at[:, mine], core_peer)
    back_own(3)
    back_other(1)
    core_add(3)
    back_own(1)
    back_other(2)
    core_add(1)
    back_own(2)
    back_other(4)
    core_add(2)
    y_add(0)
    back_own(4)
    back_other(5)
    core_add(4)
    back_own(5)
    y_add(1)
    core_add(5)
    y_add(2)
    lead_add()
    y_add(4)
    finish(0)
    y_add(5)
    finish(1)
    finish(2)
    finish(3)
    finish(4)
    finish(5)

    landed(("xsum",), slots.at[0])
    loaded(("hid",), hst.at[0])
    landed(("hidin",), hst.at[0])
    with scope("sent"):
        every = w.reshape(2 * CORES * STEPS * width, half)
        rows_sent = sent_bytes[0] // (half * w.dtype.itemsize)
        pltpu.make_async_copy(every.at[pl.ds(0, rows_sent)], every.at[pl.ds(0, rows_sent)], send_sem.at[0]).wait()


def fused_body(nz, ny, tokens, expert_ids, gate_weight, up_weight, d_hidden):
    count, features = tokens.shape
    hidden_units = gate_weight.shape[1]
    rows = d_hidden.shape[0]
    width = features // (CORES * STEPS)
    half = hidden_units // CORES
    blocks = nz * ny
    half_steps = STEPS // 2
    bf, f32 = jnp.bfloat16, jnp.float32
    loads = STEPS * 2 + 2
    recvs = STEPS * 4 + (STEPS - 1) * nz + 1 + STEPS + 3
    hbm = pl.BlockSpec(memory_space=pl.ANY)
    vmem = pl.BlockSpec(memory_space=pltpu.VMEM)
    flops = 8 * blocks * UNIT * features * half
    ids = expert_ids.T
    staged, slots, placed = pl.pallas_call(
        functools.partial(expert_kernel, nz, ny),
        out_shape=(
            pltpu.VMEM((rows, hidden_units), bf),
            pltpu.VMEM((CORES, UNIT, half_steps * width), f32),
            pltpu.VMEM((count, CORES * UNIT), f32),
        ),
        in_specs=[hbm, vmem, hbm, hbm, hbm],
        out_specs=(vmem, vmem, vmem),
        scratch_shapes=[
            pltpu.VMEM((STEPS, count, width), bf),
            pltpu.VMEM((STEPS, blocks, UNIT, width), bf),
            pltpu.VMEM((STEPS, blocks, UNIT, width), bf),
            pltpu.VMEM((STEPS, 2, 2, width, half), bf),
            pltpu.VMEM((STEPS, 2, 2, half, width), bf),
            pltpu.VMEM((2, blocks * UNIT, half), f32),
            pltpu.VMEM((2, rows, half), bf),
            pltpu.VMEM((blocks * UNIT, half), bf),
            pltpu.VMEM((blocks * UNIT, half), bf),
            pltpu.VMEM((2, rows, half), bf),
            pltpu.VMEM((STEPS, blocks * UNIT, width), bf),
            pltpu.VMEM((STEPS, blocks * UNIT, width), bf),
            pltpu.VMEM((2, blocks, UNIT, width), f32),
            pltpu.VMEM((STEPS, nz, UNIT, width), f32),
            pltpu.VMEM((STEPS, nz, UNIT, width), bf),
            pltpu.VMEM((STEPS, nz, UNIT, width), bf),
            pltpu.VMEM((STEPS, nz - 1, UNIT, width), bf),
            pltpu.VMEM((STEPS, nz - 1, UNIT, width), bf),
            pltpu.VMEM((STEPS, UNIT, width), f32),
            pltpu.VMEM((half_steps, UNIT, width), f32),
            pltpu.VMEM((nz - 1, ny, UNIT, width), bf),
            pltpu.VMEM((nz - 1, ny, UNIT, width), bf),
            pltpu.VMEM((ny, UNIT, width), f32),
            pltpu.VMEM((UNIT, width), bf),
            pltpu.VMEM((UNIT, width), bf),
            pltpu.SemaphoreType.DMA((loads,)),
            pltpu.SemaphoreType.DMA((1,)),
            pltpu.SemaphoreType.DMA((recvs,)),
        ],
        compiler_params=pltpu.CompilerParams(
            collective_id=0, has_side_effects=True, vmem_limit_bytes=62 * 1024 * 1024),
        cost_estimate=pl.CostEstimate(
            flops=flops, bytes_accessed=4 * features * half, transcendentals=0),
    )(tokens, ids, gate_weight, up_weight, d_hidden)
    d_tokens, hidden = pl.pallas_call(
        place_kernel,
        out_shape=(
            jax.ShapeDtypeStruct((count, half_steps * width), f32),
            jax.ShapeDtypeStruct((rows, hidden_units), bf),
        ),
        in_specs=[vmem, vmem, vmem],
        out_specs=(hbm, hbm),
        scratch_shapes=[
            pltpu.VMEM((half_steps, count, width), f32),
            pltpu.SemaphoreType.DMA((half_steps + 1,)),
        ],
    )(*[pltpu.with_memory_space_constraint(v, pltpu.VMEM) for v in (placed, slots, staged)])
    return hidden, d_tokens


def split_of(mesh):
    line = mesh.devices.reshape(mesh.shape["pipe"], mesh.shape["expert"])[0]
    coords = [getattr(device, "coords", None) for device in line]
    if coords[0] is None:
        return len(line) // 2, 2
    ny = len({tuple(at)[1] for at in coords})
    return len(line) // ny, ny


def solution(mesh):
    in_specs = (
        P("expert", None),
        P("expert", None),
        P(None, "expert"),
        P(None, "expert"),
        P("pipe", "expert"),
    )
    out_specs = (P("pipe", "expert"), P("expert", "pipe"))
    nz, ny = split_of(mesh)
    fits = ny == 2 and nz in (2, 4) and mesh.shape["pipe"] == 2 * CORES and 2 * UNIT == CAP
    body = functools.partial(fused_body, nz, ny) if fits else plain_body
    return jax.shard_map(body, mesh=mesh, in_specs=in_specs, out_specs=out_specs, check_vma=False)
```

```python
import functools
import math

import jax
import jax.numpy as jnp
from jax import lax
from jax.experimental import pallas as pl
from jax.experimental.pallas import tpu as pltpu
from jax.sharding import PartitionSpec as P

CAP = 32
CORES = 2
UNIT = 16
STEPS = 6
MESH_ID = pl.DeviceIdType.MESH
scope = jax.named_scope


def slot_select(expert_ids, first_slot, slot_count):
    is_named = jnp.any(expert_ids == 0, axis=1).astype(jnp.int32)
    slot_before = jnp.cumsum(is_named) - is_named
    positions = first_slot + jnp.arange(slot_count, dtype=jnp.int32)
    marked = (is_named[:, None] == 1) & (slot_before[:, None] == positions[None, :])
    return marked.astype(jnp.float32)


def plain_body(tokens, expert_ids, gate_weight, up_weight, d_hidden):
    hidden_units = gate_weight.shape[1]
    slot_span = CAP // lax.axis_size("pipe")
    own_select = slot_select(expert_ids, lax.axis_index("pipe") * slot_span, slot_span)
    routed = jnp.einsum(
        "tj,td->jd", own_select.astype(jnp.bfloat16), tokens, preferred_element_type=jnp.float32
    ).astype(jnp.bfloat16)
    piece = lax.all_gather(routed, "expert", axis=0, tiled=True)
    gate_part = jnp.dot(piece, gate_weight, preferred_element_type=jnp.float32)
    up_part = jnp.dot(piece, up_weight, preferred_element_type=jnp.float32)
    joined = jnp.concatenate([gate_part, up_part], axis=1)
    gate_value = joined[:, :hidden_units]
    up_value = joined[:, hidden_units:]
    sigmoid_gate = jax.nn.sigmoid(gate_value)
    activated = gate_value * sigmoid_gate
    hidden = (activated * up_value).astype(jnp.bfloat16)
    upstream = d_hidden.astype(jnp.float32)
    d_gate = (
        upstream * up_value * sigmoid_gate * (1.0 + gate_value * (1.0 - sigmoid_gate))
    ).astype(jnp.bfloat16)
    d_up = (upstream * activated).astype(jnp.bfloat16)
    result = jnp.einsum("nh,dh->nd", d_gate, gate_weight, preferred_element_type=jnp.float32)
    slot_grads = lax.psum_scatter(
        result + jnp.einsum("nh,dh->nd", d_up, up_weight, preferred_element_type=jnp.float32),
        "expert",
        scatter_dimension=0,
        tiled=True,
    )
    pieces = lax.all_to_all(slot_grads, "pipe", split_axis=1, concat_axis=0, tiled=True)
    full_select = slot_select(expert_ids, 0, CAP)
    d_tokens = jnp.einsum("tc,cd->td", full_select, pieces, precision=lax.Precision.HIGHEST)
    return (hidden, d_tokens)


def named_counts(ids, count):
    row_id = lax.broadcasted_iota(jnp.int32, (count, count), 0)
    col_id = lax.broadcasted_iota(jnp.int32, (count, count), 1)
    named_row = jnp.where((ids[0:1, :] == 0) | (ids[1:2, :] == 0), 1.0, 0.0)
    across = jnp.broadcast_to(named_row, (count, count))
    named_col = jnp.sum(jnp.where(row_id == col_id, across, 0.0), axis=1, keepdims=True)
    before_col = jnp.sum(jnp.where(col_id < row_id, across, 0.0), axis=1, keepdims=True)
    down = jnp.broadcast_to(named_col, (count, count))
    before_row = jnp.sum(jnp.where(row_id < col_id, down, 0.0), axis=0, keepdims=True)
    return named_row, before_row, named_col, before_col


def place_kernel(placed, slots, hid_in, dtok, hid_out, rows_out, copy_sem):
    groups, unit, features = slots.shape
    tile = rows_out.shape[2]
    hid_copy = pltpu.make_async_copy(hid_in, hid_out, copy_sem.at[0])
    hid_copy.start()
    copies = [hid_copy]
    for n in range(features // tile):
        cols = slice(n * tile, (n + 1) * tile)
        rows_out[n] = jnp.dot(
            placed[...], slots[:, :, cols].reshape(groups * unit, tile),
            precision=lax.Precision.HIGHEST, preferred_element_type=jnp.float32)
        copy = pltpu.make_async_copy(rows_out.at[n], dtok.at[:, cols], copy_sem.at[n + 1])
        copy.start()
        copies.append(copy)
    for copy in copies:
        copy.wait()


def flip(value, bit):
    return value + bit - 2 * bit * lax.rem(value // bit, 2)


def expert_kernel(nz, ny, tok, ids, gate, up, dh, hid, slots, placed,
                  tokv, own, oth, w, wt, acc, dhv, dgv, duv, hst,
                  csend, crecv, full, keep, ysend, yrecv, zsend, zrecv, fin, xsend,
                  zsend_f, zrecv_f, keep_f, ysend_f, yrecv_f,
                  load_sem, send_sem, recv_sem):
    pipe, expert = lax.axis_index("pipe"), lax.axis_index("expert")
    x, c = pipe // CORES, lax.rem(pipe, CORES)
    z, y = expert // ny, lax.rem(expert, ny)
    half_steps = STEPS // 2
    lead = half_steps
    width = tokv.shape[2]
    half = w.shape[4]
    count = tok.shape[0]
    blocks = nz * ny
    span = width * half_steps
    ring = range(1, nz)
    z_pair = {}
    for d in ring:
        other_z = z
        for k in range(nz.bit_length() - 1):
            if d >> k & 1:
                other_z = flip(other_z, 1 << k)
        z_pair[d] = other_z
    core_peer = (x * CORES + 1 - c, expert)
    x_peer = ((1 - x) * CORES + c, expert)
    y_peer = (pipe, z * ny + 1 - y)
    z_peer = {d: (pipe, z_pair[d] * ny + y) for d in ring}

    marks = {"load": {}, "recv": {}}
    sent_bytes = [0]

    def mark(kind, key):
        return marks[kind].setdefault(key, len(marks[kind]))

    def load(key, src, dst):
        pltpu.make_async_copy(src, dst, load_sem.at[mark("load", key)]).start()

    def loaded(key, ref):
        pltpu.make_async_copy(ref, ref, load_sem.at[marks["load"][key]]).wait()

    def send(key, src, dst, device):
        pltpu.make_async_remote_copy(
            src_ref=src, dst_ref=dst, send_sem=send_sem.at[0], recv_sem=recv_sem.at[mark("recv", key)],
            device_id=device, device_id_type=MESH_ID).start()
        sent_bytes[0] += math.prod(src.shape) * src.dtype.itemsize

    def landed(key, ref):
        with scope("_".join(str(k) for k in key)):
            pltpu.make_async_copy(ref, ref, recv_sem.at[marks["recv"][key]]).wait()

    def offset(other, s):
        part = c if other == 0 else 1 - c
        where = 1 - x if s < half_steps else x
        return pl.multiple_of((where * CORES + part) * span + (s % half_steps) * width, 128)

    barrier = pltpu.get_barrier_semaphore()
    peers = [core_peer, x_peer, y_peer] + [z_peer[d] for d in ring]
    for peer in peers:
        pl.semaphore_signal(barrier, inc=1, device_id=peer, device_id_type=MESH_ID)

    mine = pl.ds(pl.multiple_of(c * half, 128), half)
    others = pl.ds(pl.multiple_of((1 - c) * half, 128), half)
    for s in range(STEPS):
        load(("tok", s), tok.at[:, pl.ds(offset(0, s), width)], tokv.at[s])

    named_row, before_row, named_col, before_col = named_counts(ids, count)
    slot_id = (lax.broadcasted_iota(jnp.int32, (UNIT, count), 0) + x * UNIT).astype(jnp.float32)
    select = jnp.where((before_row == slot_id) & (named_row == 1.0), 1.0, 0.0).astype(jnp.bfloat16)

    def load_weights(s):
        for other in (0, 1):
            rows = pl.ds(offset(other, s), width)
            load(("w", s), gate.at[rows, mine], w.at[s, other, 0])
            load(("w", s), up.at[rows, mine], w.at[s, other, 1])

    weight_order = [0, lead] + [s for s in range(STEPS) if s not in (0, lead)]
    for s in weight_order[:2]:
        load_weights(s)
    with scope("barrier"):
        pl.semaphore_wait(barrier, len(peers))

    for s in range(STEPS):
        loaded(("tok", s), tokv.at[s])
        own[s, z, y] = jnp.dot(
            select, tokv[s], preferred_element_type=jnp.float32).astype(jnp.bfloat16)
        for d in ring:
            send(("zin", s), own.at[s, z, y], own.at[s, z, y], z_peer[d])
        send(("yin", s), own.at[s, z, y], own.at[s, z, y], y_peer)
        if s + 2 < STEPS:
            load_weights(weight_order[s + 2])
    load(("dh",), dh.at[:, mine], dhv.at[c])
    send(("dhin",), dh.at[:, others], dhv.at[c], core_peer)
    lane = lax.broadcasted_iota(jnp.int32, (count, CORES * UNIT), 1).astype(jnp.float32)
    placed[...] = jnp.where((before_col == lane) & (named_col == 1.0), 1.0, 0.0)

    waited, turned = set(), set()

    def weights_in(s):
        if s not in waited:
            waited.add(s)
            with scope(f"w{s}"):
                loaded(("w", s), w.at[s])

    def turn(other, s, mats=(0, 1)):
        weights_in(s)
        turned.add((other, s))
        with scope(f"turn{other}{s}"):
            for m in mats:
                wt[s, other, m] = w[s, other, m].T

    def relay(s):
        landed(("zin", s), own.at[s, pl.ds(0, nz - 1), 0])
        for d in ring:
            piece = own.at[s, z_pair[d], y]
            send(("yin", s), piece, piece, y_peer)
        send(("cin", s), own.at[s, :, y], oth.at[s, :, y], core_peer)

    def share(s):
        landed(("yin", s), own.at[s, :, 0])
        send(("cin", s), own.at[s, :, 1 - y], oth.at[s, :, 1 - y], core_peer)

    started = []

    def forward(other, s, also=()):
        weights_in(s)
        if other == 1:
            landed(("cin", s), oth.at[s])
        for _, t in also:
            weights_in(t)
        turned.update(also)
        with scope(f"fwd{other}{s}"):
            block = (own if other == 0 else oth)[s].reshape(blocks * UNIT, width)
            for m in (0, 1):
                for o, t in also:
                    wt[t, o, m] = w[t, o, m].T
                term = jnp.dot(block, w[s, other, m], preferred_element_type=jnp.float32)
                if started:
                    acc[m] += term
                else:
                    acc[m] = term
            started.append(s)

    turn(0, 0)
    turn(1, 0)
    turn(0, 3)
    turn(1, 3)
    relay(0)
    turn(1, 1)
    relay(1)
    turn(0, 1)
    turn(1, 2)
    relay(2)
    turn(0, 2)
    relay(3)
    turn(1, 4, [0])
    relay(4)
    turn(1, 4, [1])
    share(0)
    relay(5)
    forward(0, 0)
    share(1)
    forward(0, 1)
    share(2)
    forward(0, 2)
    forward(1, 0)
    share(3)
    forward(1, 1)
    forward(0, 3)
    share(4)
    forward(1, 2)
    forward(0, 4)
    share(5)
    forward(1, 3)
    forward(1, 4)
    forward(0, 5)
    forward(1, 5)

    loaded(("dh",), dhv.at[0])
    landed(("dhin",), dhv.at[0])
    tile = 256 if half % 256 == 0 else half
    with scope("epilogue"):
        for n in range(0, half, tile):
            cols = slice(n, n + tile)
            gate_value, up_value = acc[0, :, cols], acc[1, :, cols]
            first = dhv[0, :, cols].astype(jnp.float32).reshape(blocks, UNIT // 2, tile)
            second = dhv[1, :, cols].astype(jnp.float32).reshape(blocks, UNIT // 2, tile)
            upstream = jnp.stack([first, second], axis=1).reshape(blocks * UNIT, tile)
            sigmoid_gate = jax.nn.sigmoid(gate_value)
            activated = gate_value * sigmoid_gate
            hidden = (activated * up_value).reshape(blocks, 2, UNIT // 2, tile)
            for q in (0, 1):
                hst[q, :, cols] = hidden[:, q].reshape(blocks * UNIT // 2, tile).astype(jnp.bfloat16)
            dgv[:, cols] = (
                upstream * up_value * sigmoid_gate * (1.0 + gate_value * (1.0 - sigmoid_gate))
            ).astype(jnp.bfloat16)
            duv[:, cols] = (upstream * activated).astype(jnp.bfloat16)
    load(("hid",), hst.at[c], hid.at[:, mine])

    def backward(other, s):
        if (other, s) in turned:
            return jnp.dot(
                dgv[...], wt[s, other, 0], preferred_element_type=jnp.float32
            ) + jnp.dot(duv[...], wt[s, other, 1], preferred_element_type=jnp.float32)
        contract = (((1,), (1,)), ((), ()))
        return lax.dot_general(
            dgv[...], w[s, other, 0], contract, preferred_element_type=jnp.float32
        ) + lax.dot_general(duv[...], w[s, other, 1], contract, preferred_element_type=jnp.float32)

    turn_of = {}

    def back_other(s):
        turn_of[s] = len(turn_of) % 2
        with scope(f"bwd1{s}"):
            csend[s] = backward(1, s).reshape(nz, ny, UNIT, width).astype(jnp.bfloat16)
        for n in (1 - y, y):
            send(("csum", s, n is y), csend.at[s, :, n], crecv.at[s, :, n], core_peer)

    def back_own(s):
        with scope(f"bwd0{s}"):
            full[turn_of[s]] = backward(0, s).reshape(nz, ny, UNIT, width)

    def core_sum(s, where):
        return full[turn_of[s], where[0], where[1]] + crecv[s, where[0], where[1]].astype(jnp.float32)

    def core_add(s):
        landed(("csum", s, False), crecv.at[s, :, 0])
        if s == lead:
            landed(("csum", s, True), crecv.at[s, :, 0])
            for d in ring:
                for n in range(ny):
                    zsend_f[d - 1, n] = core_sum(s, (z_pair[d], n)).astype(jnp.bfloat16)
                send(("zsum", s), zsend_f.at[d - 1], zrecv_f.at[d - 1], z_peer[d])
            for n in range(ny):
                keep_f[n] = core_sum(s, (z, n))
        else:
            for d in [*ring, 0]:
                ysend[s, d] = core_sum(s, (z_pair[d] if d else z, 1 - y)).astype(jnp.bfloat16)
                send(("ysum", s, d), ysend.at[s, d], yrecv.at[s, d], y_peer)
            landed(("csum", s, True), crecv.at[s, :, 0])
            for d in [*ring, 0]:
                keep[s, d] = core_sum(s, (z_pair[d] if d else z, y))

    def lead_add():
        landed(("zsum", lead), zrecv_f)
        total = keep_f[...]
        for d in ring:
            total = total + zrecv_f[d - 1].astype(jnp.float32)
        keep_f[...] = total
        ysend_f[...] = keep_f[1 - y].astype(jnp.bfloat16)
        send(("ysum", lead), ysend_f, yrecv_f, y_peer)

    def y_add(s):
        for d in ring:
            landed(("ysum", s, d), yrecv.at[s, d])
            zsend[s, d - 1] = (keep[s, d] + yrecv[s, d].astype(jnp.float32)).astype(jnp.bfloat16)
            send(("zsum", s), zsend.at[s, d - 1], zrecv.at[s, d - 1], z_peer[d])

    def finish(s):
        if s == lead:
            landed(("ysum", s), yrecv_f)
            done = keep_f[y] + yrecv_f[...].astype(jnp.float32)
        else:
            landed(("ysum", s, 0), yrecv.at[s, 0])
            fin[s] = keep[s, 0] + yrecv[s, 0].astype(jnp.float32)
            landed(("zsum", s), zrecv.at[s])
            done = fin[s]
            for d in ring:
                done = done + zrecv[s, d - 1].astype(jnp.float32)
        cols = slice((s % half_steps) * width, (s % half_steps + 1) * width)
        if s < half_steps:
            xsend[s] = done
            send(("xsum",), xsend.at[s], slots.at[x, :, cols], x_peer)
        else:
            slots[x, :, cols] = done

    back_other(0)
    back_own(0)
    back_other(3)
    core_add(0)
    send(("hidin",), hst.at[1 - c], hid.at[:, mine], core_peer)
    back_own(3)
    back_other(1)
    core_add(3)
    back_own(1)
    back_other(2)
    core_add(1)
    back_own(2)
    back_other(4)
    core_add(2)
    y_add(0)
    back_own(4)
    back_other(5)
    core_add(4)
    back_own(5)
    y_add(1)
    core_add(5)
    y_add(2)
    lead_add()
    y_add(4)
    finish(0)
    y_add(5)
    finish(1)
    finish(2)
    finish(3)
    finish(4)
    finish(5)

    landed(("xsum",), slots.at[0])
    loaded(("hid",), hst.at[0])
    landed(("hidin",), hst.at[0])
    with scope("sent"):
        every = w.reshape(2 * CORES * STEPS * width, half)
        rows_sent = sent_bytes[0] // (half * w.dtype.itemsize)
        pltpu.make_async_copy(every.at[pl.ds(0, rows_sent)], every.at[pl.ds(0, rows_sent)], send_sem.at[0]).wait()


def fused_body(nz, ny, tokens, expert_ids, gate_weight, up_weight, d_hidden):
    count, features = tokens.shape
    hidden_units = gate_weight.shape[1]
    rows = d_hidden.shape[0]
    width = features // (CORES * STEPS)
    half = hidden_units // CORES
    blocks = nz * ny
    half_steps = STEPS // 2
    bf, f32 = jnp.bfloat16, jnp.float32
    loads = STEPS * 2 + 2
    recvs = STEPS * 5 + (STEPS - 1) * nz + 1 + STEPS + 3
    hbm = pl.BlockSpec(memory_space=pl.ANY)
    vmem = pl.BlockSpec(memory_space=pltpu.VMEM)
    flops = 8 * blocks * UNIT * features * half
    ids = expert_ids.T
    staged, slots, placed = pl.pallas_call(
        functools.partial(expert_kernel, nz, ny),
        out_shape=(
            pltpu.VMEM((rows, hidden_units), bf),
            pltpu.VMEM((CORES, UNIT, half_steps * width), f32),
            pltpu.VMEM((count, CORES * UNIT), f32),
        ),
        in_specs=[hbm, vmem, hbm, hbm, hbm],
        out_specs=(vmem, vmem, vmem),
        scratch_shapes=[
            pltpu.VMEM((STEPS, count, width), bf),
            pltpu.VMEM((STEPS, nz, ny, UNIT, width), bf),
            pltpu.VMEM((STEPS, nz, ny, UNIT, width), bf),
            pltpu.VMEM((STEPS, 2, 2, width, half), bf),
            pltpu.VMEM((STEPS, 2, 2, half, width), bf),
            pltpu.VMEM((2, blocks * UNIT, half), f32),
            pltpu.VMEM((2, rows, half), bf),
            pltpu.VMEM((blocks * UNIT, half), bf),
            pltpu.VMEM((blocks * UNIT, half), bf),
            pltpu.VMEM((2, rows, half), bf),
            pltpu.VMEM((STEPS, nz, ny, UNIT, width), bf),
            pltpu.VMEM((STEPS, nz, ny, UNIT, width), bf),
            pltpu.VMEM((2, nz, ny, UNIT, width), f32),
            pltpu.VMEM((STEPS, nz, UNIT, width), f32),
            pltpu.VMEM((STEPS, nz, UNIT, width), bf),
            pltpu.VMEM((STEPS, nz, UNIT, width), bf),
            pltpu.VMEM((STEPS, nz - 1, UNIT, width), bf),
            pltpu.VMEM((STEPS, nz - 1, UNIT, width), bf),
            pltpu.VMEM((STEPS, UNIT, width), f32),
            pltpu.VMEM((half_steps, UNIT, width), f32),
            pltpu.VMEM((nz - 1, ny, UNIT, width), bf),
            pltpu.VMEM((nz - 1, ny, UNIT, width), bf),
            pltpu.VMEM((ny, UNIT, width), f32),
            pltpu.VMEM((UNIT, width), bf),
            pltpu.VMEM((UNIT, width), bf),
            pltpu.SemaphoreType.DMA((loads,)),
            pltpu.SemaphoreType.DMA((1,)),
            pltpu.SemaphoreType.DMA((recvs,)),
        ],
        compiler_params=pltpu.CompilerParams(
            collective_id=0, has_side_effects=True, vmem_limit_bytes=62 * 1024 * 1024),
        cost_estimate=pl.CostEstimate(
            flops=flops, bytes_accessed=4 * features * half, transcendentals=0),
    )(tokens, ids, gate_weight, up_weight, d_hidden)
    d_tokens, hidden = pl.pallas_call(
        place_kernel,
        out_shape=(
            jax.ShapeDtypeStruct((count, half_steps * width), f32),
            jax.ShapeDtypeStruct((rows, hidden_units), bf),
        ),
        in_specs=[vmem, vmem, vmem],
        out_specs=(hbm, hbm),
        scratch_shapes=[
            pltpu.VMEM((half_steps, count, width), f32),
            pltpu.SemaphoreType.DMA((half_steps + 1,)),
        ],
    )(*[pltpu.with_memory_space_constraint(v, pltpu.VMEM) for v in (placed, slots, staged)])
    return hidden, d_tokens


def split_of(mesh):
    line = mesh.devices.reshape(mesh.shape["pipe"], mesh.shape["expert"])[0]
    coords = [getattr(device, "coords", None) for device in line]
    if coords[0] is None:
        return len(line) // 2, 2
    ny = len({tuple(at)[1] for at in coords})
    return len(line) // ny, ny


def solution(mesh):
    in_specs = (
        P("expert", None),
        P("expert", None),
        P(None, "expert"),
        P(None, "expert"),
        P("pipe", "expert"),
    )
    out_specs = (P("pipe", "expert"), P("expert", "pipe"))
    nz, ny = split_of(mesh)
    fits = ny == 2 and nz in (2, 4) and mesh.shape["pipe"] == 2 * CORES and 2 * UNIT == CAP
    body = functools.partial(fused_body, nz, ny) if fits else plain_body
    return jax.shard_map(body, mesh=mesh, in_specs=in_specs, out_specs=out_specs, check_vma=False)
```

```python
import functools
import math

import jax
import jax.numpy as jnp
from jax import lax
from jax.experimental import pallas as pl
from jax.experimental.pallas import tpu as pltpu
from jax.sharding import PartitionSpec as P

CAP = 32
CORES = 2
UNIT = 16
STEPS = 6
MESH_ID = pl.DeviceIdType.MESH
scope = jax.named_scope


def slot_select(expert_ids, first_slot, slot_count):
    is_named = jnp.any(expert_ids == 0, axis=1).astype(jnp.int32)
    slot_before = jnp.cumsum(is_named) - is_named
    positions = first_slot + jnp.arange(slot_count, dtype=jnp.int32)
    marked = (is_named[:, None] == 1) & (slot_before[:, None] == positions[None, :])
    return marked.astype(jnp.float32)


def plain_body(tokens, expert_ids, gate_weight, up_weight, d_hidden):
    hidden_units = gate_weight.shape[1]
    slot_span = CAP // lax.axis_size("pipe")
    own_select = slot_select(expert_ids, lax.axis_index("pipe") * slot_span, slot_span)
    routed = jnp.einsum(
        "tj,td->jd", own_select.astype(jnp.bfloat16), tokens, preferred_element_type=jnp.float32
    ).astype(jnp.bfloat16)
    piece = lax.all_gather(routed, "expert", axis=0, tiled=True)
    gate_part = jnp.dot(piece, gate_weight, preferred_element_type=jnp.float32)
    up_part = jnp.dot(piece, up_weight, preferred_element_type=jnp.float32)
    joined = jnp.concatenate([gate_part, up_part], axis=1)
    gate_value = joined[:, :hidden_units]
    up_value = joined[:, hidden_units:]
    sigmoid_gate = jax.nn.sigmoid(gate_value)
    activated = gate_value * sigmoid_gate
    hidden = (activated * up_value).astype(jnp.bfloat16)
    upstream = d_hidden.astype(jnp.float32)
    d_gate = (
        upstream * up_value * sigmoid_gate * (1.0 + gate_value * (1.0 - sigmoid_gate))
    ).astype(jnp.bfloat16)
    d_up = (upstream * activated).astype(jnp.bfloat16)
    result = jnp.einsum("nh,dh->nd", d_gate, gate_weight, preferred_element_type=jnp.float32)
    slot_grads = lax.psum_scatter(
        result + jnp.einsum("nh,dh->nd", d_up, up_weight, preferred_element_type=jnp.float32),
        "expert",
        scatter_dimension=0,
        tiled=True,
    )
    pieces = lax.all_to_all(slot_grads, "pipe", split_axis=1, concat_axis=0, tiled=True)
    full_select = slot_select(expert_ids, 0, CAP)
    d_tokens = jnp.einsum("tc,cd->td", full_select, pieces, precision=lax.Precision.HIGHEST)
    return (hidden, d_tokens)


def named_counts(ids, count):
    row_id = lax.broadcasted_iota(jnp.int32, (count, count), 0)
    col_id = lax.broadcasted_iota(jnp.int32, (count, count), 1)
    named_row = jnp.where((ids[0:1, :] == 0) | (ids[1:2, :] == 0), 1.0, 0.0)
    across = jnp.broadcast_to(named_row, (count, count))
    named_col = jnp.sum(jnp.where(row_id == col_id, across, 0.0), axis=1, keepdims=True)
    before_col = jnp.sum(jnp.where(col_id < row_id, across, 0.0), axis=1, keepdims=True)
    down = jnp.broadcast_to(named_col, (count, count))
    before_row = jnp.sum(jnp.where(row_id < col_id, down, 0.0), axis=0, keepdims=True)
    return named_row, before_row, named_col, before_col


def place_kernel(placed, slots, hid_in, dtok, hid_out, rows_out, copy_sem):
    groups, unit, features = slots.shape
    tile = rows_out.shape[2]
    hid_copy = pltpu.make_async_copy(hid_in, hid_out, copy_sem.at[0])
    hid_copy.start()
    copies = [hid_copy]
    chosen = jnp.concatenate([placed[...].astype(jnp.bfloat16)] * 3, axis=1)
    for n in range(features // tile):
        cols = slice(n * tile, (n + 1) * tile)
        rest = slots[:, :, cols].reshape(groups * unit, tile)
        parts = []
        for _ in range(3):
            parts.append(rest.astype(jnp.bfloat16))
            rest = rest - parts[-1].astype(jnp.float32)
        rows_out[n] = jnp.dot(
            chosen, jnp.concatenate(parts, axis=0), preferred_element_type=jnp.float32)
        copy = pltpu.make_async_copy(rows_out.at[n], dtok.at[:, cols], copy_sem.at[n + 1])
        copy.start()
        copies.append(copy)
    for copy in copies:
        copy.wait()


def expert_kernel(nz, ny, tok, ids, gate, up, dh, hid, slots, placed,
                  tokv, own, oth, w, wt, acc, dhv, dgv, duv, hst,
                  csend, crecv, full, keep, ysend, yrecv, zsend, zrecv, xsend, xrecv,
                  zsend_f, zrecv_f, keep_f, ysend_f, yrecv_f,
                  load_sem, send_sem, recv_sem):
    pipe, expert = lax.axis_index("pipe"), lax.axis_index("expert")
    x, c = pipe // CORES, lax.rem(pipe, CORES)
    z, y = expert // ny, lax.rem(expert, ny)
    half_steps = STEPS // 2
    lead = half_steps
    width = tokv.shape[2]
    half = w.shape[4]
    count = tok.shape[0]
    blocks = nz * ny
    span = width * half_steps
    ring = range(1, nz)
    z_pair = {d: d - 1 + (d - 1 - z + nz) // nz for d in ring}
    z_slot = {d: z - (z - z_pair[d] - 1 + nz) // nz for d in ring}
    core_peer = (x * CORES + 1 - c, expert)
    x_peer = ((1 - x) * CORES + c, expert)
    y_peer = (pipe, z * ny + 1 - y)
    z_peer = {d: (pipe, z_pair[d] * ny + y) for d in ring}
    xz_peer = {d: ((1 - x) * CORES + c, z_pair[d] * ny + y) for d in ring}

    marks = {"load": {}, "recv": {}}
    sent_bytes = [0]

    def mark(kind, key):
        return marks[kind].setdefault(key, len(marks[kind]))

    def load(key, src, dst):
        pltpu.make_async_copy(src, dst, load_sem.at[mark("load", key)]).start()

    def loaded(key, ref):
        pltpu.make_async_copy(ref, ref, load_sem.at[marks["load"][key]]).wait()

    def send(key, src, dst, device):
        pltpu.make_async_remote_copy(
            src_ref=src, dst_ref=dst, send_sem=send_sem.at[0], recv_sem=recv_sem.at[mark("recv", key)],
            device_id=device, device_id_type=MESH_ID).start()
        sent_bytes[0] += math.prod(src.shape) * src.dtype.itemsize

    def landed(key, ref):
        with scope("_".join(str(k) for k in key)):
            pltpu.make_async_copy(ref, ref, recv_sem.at[marks["recv"][key]]).wait()

    def offset(other, s):
        part = c if other == 0 else 1 - c
        where = 1 - x if s < half_steps else x
        return pl.multiple_of((where * CORES + part) * span + (s % half_steps) * width, 128)

    barrier = pltpu.get_barrier_semaphore()
    peers = [core_peer, x_peer, y_peer, *z_peer.values(), *xz_peer.values()]
    for peer in peers:
        pl.semaphore_signal(barrier, inc=1, device_id=peer, device_id_type=MESH_ID)

    mine = pl.ds(pl.multiple_of(c * half, 128), half)
    others = pl.ds(pl.multiple_of((1 - c) * half, 128), half)
    for s in range(STEPS):
        load(("tok", s), tok.at[:, pl.ds(offset(0, s), width)], tokv.at[s])

    named_row, before_row, named_col, before_col = named_counts(ids, count)
    slot_id = (lax.broadcasted_iota(jnp.int32, (UNIT, count), 0) + x * UNIT).astype(jnp.float32)
    select = jnp.where((before_row == slot_id) & (named_row == 1.0), 1.0, 0.0).astype(jnp.bfloat16)

    def load_weights(s):
        for other in (0, 1):
            rows = pl.ds(offset(other, s), width)
            load(("w", s), gate.at[rows, mine], w.at[s, other, 0])
            load(("w", s), up.at[rows, mine], w.at[s, other, 1])

    weight_order = [0, lead] + [s for s in range(STEPS) if s not in (0, lead)]
    for s in weight_order[:2]:
        load_weights(s)
    with scope("barrier"):
        pl.semaphore_wait(barrier, len(peers))

    def own_out(s):
        loaded(("tok", s), tokv.at[s])
        own[s, z, y] = jnp.dot(
            select, tokv[s], preferred_element_type=jnp.float32).astype(jnp.bfloat16)
        for d in ring:
            send(("zin", s), own.at[s, z, y], own.at[s, z, y], z_peer[d])
        send(("yin", s), own.at[s, z, y], own.at[s, z, y], y_peer)

    own_out(0)
    for s in weight_order[2:]:
        load_weights(s)
    load(("dh",), dh.at[:, mine], dhv.at[c])
    send(("dhin",), dh.at[:, others], dhv.at[c], core_peer)
    lane = lax.broadcasted_iota(jnp.int32, (count, CORES * UNIT), 1).astype(jnp.float32)
    placed[...] = jnp.where((before_col == lane) & (named_col == 1.0), 1.0, 0.0)

    waited, turned = set(), set()

    def weights_in(s):
        if s not in waited:
            waited.add(s)
            with scope(f"w{s}"):
                loaded(("w", s), w.at[s])

    def turn(other, s, mats=(0, 1)):
        weights_in(s)
        turned.add((other, s))
        with scope(f"turn{other}{s}"):
            for m in mats:
                wt[s, other, m] = w[s, other, m].T

    def relay(s):
        landed(("zin", s), own.at[s, pl.ds(0, nz - 1), 0])
        for d in ring:
            piece = own.at[s, z_pair[d], y]
            send(("yin", s), piece, piece, y_peer)
        send(("cin", s), own.at[s, :, y], oth.at[s, :, y], core_peer)

    def share(s):
        landed(("yin", s), own.at[s, :, 0])
        send(("cin", s), own.at[s, :, 1 - y], oth.at[s, :, 1 - y], core_peer)

    started = []

    def forward(other, s, also=()):
        weights_in(s)
        if other == 1:
            landed(("cin", s), oth.at[s])
        for _, t in also:
            weights_in(t)
        turned.update(also)
        with scope(f"fwd{other}{s}"):
            block = (own if other == 0 else oth)[s].reshape(blocks * UNIT, width)
            for m in (0, 1):
                for o, t in also:
                    wt[t, o, m] = w[t, o, m].T
                term = jnp.dot(block, w[s, other, m], preferred_element_type=jnp.float32)
                if started:
                    acc[m] += term
                else:
                    acc[m] = term
            started.append(s)

    own_out(1)
    own_out(2)
    turn(0, 0)
    own_out(3)
    turn(1, 0)
    own_out(4)
    turn(0, 3)
    own_out(5)
    turn(1, 3)
    relay(0)
    turn(1, 1)
    relay(1)
    turn(0, 1)
    turn(1, 2)
    relay(2)
    turn(0, 2)
    relay(3)
    turn(1, 4, [0])
    relay(4)
    turn(1, 4, [1])
    share(0)
    relay(5)
    forward(0, 0)
    share(1)
    forward(0, 1)
    share(2)
    forward(0, 2)
    forward(1, 0)
    share(3)
    forward(1, 1)
    forward(0, 3)
    share(4)
    forward(1, 2)
    forward(0, 4)
    share(5)
    forward(1, 3)
    forward(1, 4)
    forward(0, 5)
    forward(1, 5)

    loaded(("dh",), dhv.at[0])
    landed(("dhin",), dhv.at[0])
    tile = 256 if half % 256 == 0 else half
    with scope("epilogue"):
        for n in range(0, half, tile):
            cols = slice(n, n + tile)
            gate_value, up_value = acc[0, :, cols], acc[1, :, cols]
            first = dhv[0, :, cols].astype(jnp.float32).reshape(blocks, UNIT // 2, tile)
            second = dhv[1, :, cols].astype(jnp.float32).reshape(blocks, UNIT // 2, tile)
            upstream = jnp.stack([first, second], axis=1).reshape(blocks * UNIT, tile)
            sigmoid_gate = jax.nn.sigmoid(gate_value)
            activated = gate_value * sigmoid_gate
            hidden = (activated * up_value).reshape(blocks, 2, UNIT // 2, tile)
            for q in (0, 1):
                hst[q, :, cols] = hidden[:, q].reshape(blocks * UNIT // 2, tile).astype(jnp.bfloat16)
            dgv[:, cols] = (
                upstream * up_value * sigmoid_gate * (1.0 + gate_value * (1.0 - sigmoid_gate))
            ).astype(jnp.bfloat16)
            duv[:, cols] = (upstream * activated).astype(jnp.bfloat16)
    load(("hid",), hst.at[c], hid.at[:, mine])

    def backward(other, s):
        if (other, s) in turned:
            return jnp.dot(
                dgv[...], wt[s, other, 0], preferred_element_type=jnp.float32
            ) + jnp.dot(duv[...], wt[s, other, 1], preferred_element_type=jnp.float32)
        contract = (((1,), (1,)), ((), ()))
        return lax.dot_general(
            dgv[...], w[s, other, 0], contract, preferred_element_type=jnp.float32
        ) + lax.dot_general(duv[...], w[s, other, 1], contract, preferred_element_type=jnp.float32)

    turn_of = {}

    def back_other(s):
        turn_of[s] = len(turn_of) % 2
        with scope(f"bwd1{s}"):
            csend[s] = backward(1, s).reshape(nz, ny, UNIT, width).astype(jnp.bfloat16)
        for n in (1 - y, y):
            send(("csum", s, n is y), csend.at[s, :, n], crecv.at[s, :, n], core_peer)

    def back_own(s):
        with scope(f"bwd0{s}"):
            full[turn_of[s]] = backward(0, s).reshape(nz, ny, UNIT, width)

    def core_sum(s, where):
        return full[turn_of[s], where[0], where[1]] + crecv[s, where[0], where[1]].astype(jnp.float32)

    def core_add(s):
        landed(("csum", s, False), crecv.at[s, :, 0])
        if s == lead:
            landed(("csum", s, True), crecv.at[s, :, 0])
            for d in ring:
                for n in range(ny):
                    zsend_f[d - 1, n] = core_sum(s, (z_pair[d], n)).astype(jnp.bfloat16)
                send(("zsum", s), zsend_f.at[d - 1], zrecv_f.at[z_slot[d]], z_peer[d])
            for n in range(ny):
                keep_f[n] = core_sum(s, (z, n))
        else:
            for d in [*ring, 0]:
                ysend[s, d] = core_sum(s, (z_pair[d] if d else z, 1 - y)).astype(jnp.bfloat16)
                send(("ysum", s, d), ysend.at[s, d], yrecv.at[s, d], y_peer)
            landed(("csum", s, True), crecv.at[s, :, 0])
            for d in [*ring, 0]:
                keep[s, d] = core_sum(s, (z_pair[d] if d else z, y))

    def lead_add():
        landed(("zsum", lead), zrecv_f)
        total = keep_f[...]
        for d in ring:
            total = total + zrecv_f[d - 1].astype(jnp.float32)
        keep_f[...] = total
        ysend_f[...] = keep_f[1 - y].astype(jnp.bfloat16)
        send(("ysum", lead), ysend_f, yrecv_f, y_peer)

    def y_sum(s, d):
        landed(("ysum", s, d), yrecv.at[s, d])
        return keep[s, d] + yrecv[s, d].astype(jnp.float32)

    def y_add(s):
        for d in ring:
            zsend[s, d - 1] = y_sum(s, d).astype(jnp.bfloat16)
            send(("zsum", s), zsend.at[s, d - 1], zrecv.at[s, z_slot[d]],
                 (xz_peer if s < half_steps else z_peer)[d])

    def hand_over(s):
        xsend[s] = y_sum(s, 0)
        send(("xsum", s), xsend.at[s], xrecv.at[s], x_peer)

    def finish(s):
        if s == lead:
            landed(("ysum", s), yrecv_f)
            done = keep_f[y] + yrecv_f[...].astype(jnp.float32)
        else:
            if s < half_steps:
                landed(("xsum", s), xrecv.at[s])
                done = xrecv[s]
            else:
                done = y_sum(s, 0)
            landed(("zsum", s), zrecv.at[s])
            for d in ring:
                done = done + zrecv[s, d - 1].astype(jnp.float32)
        cols = slice((s % half_steps) * width, (s % half_steps + 1) * width)
        slots[1 - x if s < half_steps else x, :, cols] = done

    back_other(0)
    back_own(0)
    back_other(3)
    core_add(0)
    send(("hidin",), hst.at[1 - c], hid.at[:, mine], core_peer)
    back_own(3)
    back_other(1)
    core_add(3)
    back_own(1)
    back_other(2)
    core_add(1)
    back_own(2)
    back_other(4)
    core_add(2)
    y_add(0)
    hand_over(0)
    back_own(4)
    back_other(5)
    core_add(4)
    back_own(5)
    y_add(1)
    hand_over(1)
    core_add(5)
    y_add(2)
    hand_over(2)
    lead_add()
    y_add(4)
    y_add(5)
    finish(0)
    finish(1)
    finish(2)
    finish(3)
    finish(4)
    finish(5)

    loaded(("hid",), hst.at[0])
    landed(("hidin",), hst.at[0])
    with scope("sent"):
        every = w.reshape(2 * CORES * STEPS * width, half)
        rows_sent = sent_bytes[0] // (half * w.dtype.itemsize)
        pltpu.make_async_copy(every.at[pl.ds(0, rows_sent)], every.at[pl.ds(0, rows_sent)], send_sem.at[0]).wait()


def fused_body(nz, ny, tokens, expert_ids, gate_weight, up_weight, d_hidden):
    count, features = tokens.shape
    hidden_units = gate_weight.shape[1]
    rows = d_hidden.shape[0]
    width = features // (CORES * STEPS)
    half = hidden_units // CORES
    blocks = nz * ny
    half_steps = STEPS // 2
    bf, f32 = jnp.bfloat16, jnp.float32
    loads = STEPS * 2 + 2
    recvs = STEPS * 5 + (STEPS - 1) * nz + 1 + STEPS + 5
    hbm = pl.BlockSpec(memory_space=pl.ANY)
    vmem = pl.BlockSpec(memory_space=pltpu.VMEM)
    flops = 8 * blocks * UNIT * features * half
    ids = expert_ids.T
    staged, slots, placed = pl.pallas_call(
        functools.partial(expert_kernel, nz, ny),
        out_shape=(
            pltpu.VMEM((rows, hidden_units), bf),
            pltpu.VMEM((CORES, UNIT, half_steps * width), f32),
            pltpu.VMEM((count, CORES * UNIT), f32),
        ),
        in_specs=[hbm, vmem, hbm, hbm, hbm],
        out_specs=(vmem, vmem, vmem),
        scratch_shapes=[
            pltpu.VMEM((STEPS, count, width), bf),
            pltpu.VMEM((STEPS, nz, ny, UNIT, width), bf),
            pltpu.VMEM((STEPS, nz, ny, UNIT, width), bf),
            pltpu.VMEM((STEPS, 2, 2, width, half), bf),
            pltpu.VMEM((STEPS, 2, 2, half, width), bf),
            pltpu.VMEM((2, blocks * UNIT, half), f32),
            pltpu.VMEM((2, rows, half), bf),
            pltpu.VMEM((blocks * UNIT, half), bf),
            pltpu.VMEM((blocks * UNIT, half), bf),
            pltpu.VMEM((2, rows, half), bf),
            pltpu.VMEM((STEPS, nz, ny, UNIT, width), bf),
            pltpu.VMEM((STEPS, nz, ny, UNIT, width), bf),
            pltpu.VMEM((2, nz, ny, UNIT, width), f32),
            pltpu.VMEM((STEPS, nz, UNIT, width), f32),
            pltpu.VMEM((STEPS, nz, UNIT, width), bf),
            pltpu.VMEM((STEPS, nz, UNIT, width), bf),
            pltpu.VMEM((STEPS, nz - 1, UNIT, width), bf),
            pltpu.VMEM((STEPS, nz - 1, UNIT, width), bf),
            pltpu.VMEM((half_steps, UNIT, width), f32),
            pltpu.VMEM((half_steps, UNIT, width), f32),
            pltpu.VMEM((nz - 1, ny, UNIT, width), bf),
            pltpu.VMEM((nz - 1, ny, UNIT, width), bf),
            pltpu.VMEM((ny, UNIT, width), f32),
            pltpu.VMEM((UNIT, width), bf),
            pltpu.VMEM((UNIT, width), bf),
            pltpu.SemaphoreType.DMA((loads,)),
            pltpu.SemaphoreType.DMA((1,)),
            pltpu.SemaphoreType.DMA((recvs,)),
        ],
        compiler_params=pltpu.CompilerParams(
            collective_id=0, has_side_effects=True, vmem_limit_bytes=62 * 1024 * 1024),
        cost_estimate=pl.CostEstimate(
            flops=flops, bytes_accessed=4 * features * half, transcendentals=0),
    )(tokens, ids, gate_weight, up_weight, d_hidden)
    d_tokens, hidden = pl.pallas_call(
        place_kernel,
        out_shape=(
            jax.ShapeDtypeStruct((count, half_steps * width), f32),
            jax.ShapeDtypeStruct((rows, hidden_units), bf),
        ),
        in_specs=[vmem, vmem, vmem],
        out_specs=(hbm, hbm),
        scratch_shapes=[
            pltpu.VMEM((half_steps, count, width), f32),
            pltpu.SemaphoreType.DMA((half_steps + 1,)),
        ],
    )(*[pltpu.with_memory_space_constraint(v, pltpu.VMEM) for v in (placed, slots, staged)])
    return hidden, d_tokens


def split_of(mesh):
    line = mesh.devices.reshape(mesh.shape["pipe"], mesh.shape["expert"])[0]
    coords = [getattr(device, "coords", None) for device in line]
    if coords[0] is None:
        return len(line) // 2, 2
    ny = len({tuple(at)[1] for at in coords})
    return len(line) // ny, ny


def solution(mesh):
    in_specs = (
        P("expert", None),
        P("expert", None),
        P(None, "expert"),
        P(None, "expert"),
        P("pipe", "expert"),
    )
    out_specs = (P("pipe", "expert"), P("expert", "pipe"))
    nz, ny = split_of(mesh)
    fits = ny == 2 and nz in (2, 4) and mesh.shape["pipe"] == 2 * CORES and 2 * UNIT == CAP
    body = functools.partial(fused_body, nz, ny) if fits else plain_body
    return jax.shard_map(body, mesh=mesh, in_specs=in_specs, out_specs=out_specs, check_vma=False)
```

```python
import functools
import math

import jax
import jax.numpy as jnp
from jax import lax
from jax.experimental import pallas as pl
from jax.experimental.pallas import tpu as pltpu
from jax.sharding import PartitionSpec as P

CAP = 32
CORES = 2
UNIT = 16
STEPS = 6
MESH_ID = pl.DeviceIdType.MESH
scope = jax.named_scope


def slot_select(expert_ids, first_slot, slot_count):
    is_named = jnp.any(expert_ids == 0, axis=1).astype(jnp.int32)
    slot_before = jnp.cumsum(is_named) - is_named
    positions = first_slot + jnp.arange(slot_count, dtype=jnp.int32)
    marked = (is_named[:, None] == 1) & (slot_before[:, None] == positions[None, :])
    return marked.astype(jnp.float32)


def plain_body(tokens, expert_ids, gate_weight, up_weight, d_hidden):
    hidden_units = gate_weight.shape[1]
    slot_span = CAP // lax.axis_size("pipe")
    own_select = slot_select(expert_ids, lax.axis_index("pipe") * slot_span, slot_span)
    routed = jnp.einsum(
        "tj,td->jd", own_select.astype(jnp.bfloat16), tokens, preferred_element_type=jnp.float32
    ).astype(jnp.bfloat16)
    piece = lax.all_gather(routed, "expert", axis=0, tiled=True)
    gate_part = jnp.dot(piece, gate_weight, preferred_element_type=jnp.float32)
    up_part = jnp.dot(piece, up_weight, preferred_element_type=jnp.float32)
    joined = jnp.concatenate([gate_part, up_part], axis=1)
    gate_value = joined[:, :hidden_units]
    up_value = joined[:, hidden_units:]
    sigmoid_gate = jax.nn.sigmoid(gate_value)
    activated = gate_value * sigmoid_gate
    hidden = (activated * up_value).astype(jnp.bfloat16)
    upstream = d_hidden.astype(jnp.float32)
    d_gate = (
        upstream * up_value * sigmoid_gate * (1.0 + gate_value * (1.0 - sigmoid_gate))
    ).astype(jnp.bfloat16)
    d_up = (upstream * activated).astype(jnp.bfloat16)
    result = jnp.einsum("nh,dh->nd", d_gate, gate_weight, preferred_element_type=jnp.float32)
    slot_grads = lax.psum_scatter(
        result + jnp.einsum("nh,dh->nd", d_up, up_weight, preferred_element_type=jnp.float32),
        "expert",
        scatter_dimension=0,
        tiled=True,
    )
    pieces = lax.all_to_all(slot_grads, "pipe", split_axis=1, concat_axis=0, tiled=True)
    full_select = slot_select(expert_ids, 0, CAP)
    d_tokens = jnp.einsum("tc,cd->td", full_select, pieces, precision=lax.Precision.HIGHEST)
    return (hidden, d_tokens)


def named_counts(ids, count):
    row_id = lax.broadcasted_iota(jnp.int32, (count, count), 0)
    col_id = lax.broadcasted_iota(jnp.int32, (count, count), 1)
    named_row = jnp.where((ids[0:1, :] == 0) | (ids[1:2, :] == 0), 1.0, 0.0)
    across = jnp.broadcast_to(named_row, (count, count))
    named_col = jnp.sum(jnp.where(row_id == col_id, across, 0.0), axis=1, keepdims=True)
    before_col = jnp.sum(jnp.where(col_id < row_id, across, 0.0), axis=1, keepdims=True)
    down = jnp.broadcast_to(named_col, (count, count))
    before_row = jnp.sum(jnp.where(row_id < col_id, down, 0.0), axis=0, keepdims=True)
    return named_row, before_row, named_col, before_col


def place_kernel(placed, slots, hid_in, dtok, hid_out, rows_out, copy_sem):
    groups, unit, features = slots.shape
    tile = rows_out.shape[2]
    hid_copy = pltpu.make_async_copy(hid_in, hid_out, copy_sem.at[0])
    hid_copy.start()
    copies = [hid_copy]
    chosen = jnp.concatenate([placed[...].astype(jnp.bfloat16)] * 3, axis=1)
    for n in range(features // tile):
        cols = slice(n * tile, (n + 1) * tile)
        rest = slots[:, :, cols].reshape(groups * unit, tile)
        parts = []
        for _ in range(3):
            parts.append(rest.astype(jnp.bfloat16))
            rest = rest - parts[-1].astype(jnp.float32)
        rows_out[n] = jnp.dot(
            chosen, jnp.concatenate(parts, axis=0), preferred_element_type=jnp.float32)
        copy = pltpu.make_async_copy(rows_out.at[n], dtok.at[:, cols], copy_sem.at[n + 1])
        copy.start()
        copies.append(copy)
    for copy in copies:
        copy.wait()


def expert_kernel(nz, ny, tok, ids, gate, up, dh, hid, slots, placed,
                  tokv, own, oth, w, wt, acc, dhv, dgv, duv, hst,
                  csend, crecv, full, keep, ysend, yrecv, zsend, zrecv, xsend, xrecv,
                  zsend_f, zrecv_f, keep_f, ysend_f, yrecv_f,
                  load_sem, send_sem, recv_sem):
    pipe, expert = lax.axis_index("pipe"), lax.axis_index("expert")
    x, c = pipe // CORES, lax.rem(pipe, CORES)
    z, y = expert // ny, lax.rem(expert, ny)
    half_steps = STEPS // 2
    lead = half_steps
    width = tokv.shape[2]
    half = w.shape[4]
    count = tok.shape[0]
    blocks = nz * ny
    span = width * half_steps
    ring = range(1, nz)
    z_pair = {d: d - 1 + (d - 1 - z + nz) // nz for d in ring}
    z_slot = {d: z - (z - z_pair[d] - 1 + nz) // nz for d in ring}
    core_peer = (x * CORES + 1 - c, expert)
    x_peer = ((1 - x) * CORES + c, expert)
    y_peer = (pipe, z * ny + 1 - y)
    z_peer = {d: (pipe, z_pair[d] * ny + y) for d in ring}
    xz_peer = {d: ((1 - x) * CORES + c, z_pair[d] * ny + y) for d in ring}

    marks = {"load": {}, "recv": {}}
    sent_bytes = [0]

    def reuse(key):
        if key[0] == "ysum" and key[2:] in ((), (1,)):
            return ("zin", key[1])
        return ("yin", key[1]) if key[0] == "csum" and not key[2] else key

    def mark(kind, key):
        return marks[kind].setdefault(reuse(key), len(marks[kind]))

    def load(key, src, dst):
        pltpu.make_async_copy(src, dst, load_sem.at[mark("load", key)]).start()

    def loaded(key, ref):
        pltpu.make_async_copy(ref, ref, load_sem.at[marks["load"][key]]).wait()

    def send(key, src, dst, device):
        pltpu.make_async_remote_copy(
            src_ref=src, dst_ref=dst, send_sem=send_sem.at[0], recv_sem=recv_sem.at[mark("recv", key)],
            device_id=device, device_id_type=MESH_ID).start()
        sent_bytes[0] += math.prod(src.shape) * src.dtype.itemsize

    def landed(key, ref):
        with scope("_".join(str(k) for k in key)):
            pltpu.make_async_copy(ref, ref, recv_sem.at[marks["recv"][reuse(key)]]).wait()

    def offset(other, s):
        part = c if other == 0 else 1 - c
        where = 1 - x if s < half_steps else x
        return pl.multiple_of((where * CORES + part) * span + (s % half_steps) * width, 128)

    barrier = pltpu.get_barrier_semaphore()
    peers = [core_peer, x_peer, y_peer, *z_peer.values(), *xz_peer.values()]
    for peer in peers:
        pl.semaphore_signal(barrier, inc=1, device_id=peer, device_id_type=MESH_ID)

    mine = pl.ds(pl.multiple_of(c * half, 128), half)
    others = pl.ds(pl.multiple_of((1 - c) * half, 128), half)
    for s in range(STEPS):
        load(("tok", s), tok.at[:, pl.ds(offset(0, s), width)], tokv.at[s])

    named_row, before_row, named_col, before_col = named_counts(ids, count)
    slot_id = (lax.broadcasted_iota(jnp.int32, (UNIT, count), 0) + x * UNIT).astype(jnp.float32)
    select = jnp.where((before_row == slot_id) & (named_row == 1.0), 1.0, 0.0).astype(jnp.bfloat16)

    def load_weights(s):
        for other in (0, 1):
            rows = pl.ds(offset(other, s), width)
            load(("w", s), gate.at[rows, mine], w.at[s, other, 0])
            load(("w", s), up.at[rows, mine], w.at[s, other, 1])

    weight_order = [0, lead] + [s for s in range(STEPS) if s not in (0, lead)]
    for s in weight_order[:2]:
        load_weights(s)
    with scope("barrier"):
        pl.semaphore_wait(barrier, len(peers))

    def own_out(s):
        loaded(("tok", s), tokv.at[s])
        own[s, z, y] = jnp.dot(
            select, tokv[s], preferred_element_type=jnp.float32).astype(jnp.bfloat16)
        for d in ring:
            send(("zin", s), own.at[s, z, y], own.at[s, z, y], z_peer[d])
        send(("yin", s), own.at[s, z, y], own.at[s, z, y], y_peer)

    own_out(0)
    for s in weight_order[2:]:
        load_weights(s)
    load(("dh",), dh.at[:, mine], dhv.at[c])
    send(("dhin",), dh.at[:, others], dhv.at[c], core_peer)
    lane = lax.broadcasted_iota(jnp.int32, (count, CORES * UNIT), 1).astype(jnp.float32)
    placed[...] = jnp.where((before_col == lane) & (named_col == 1.0), 1.0, 0.0)

    waited, turned = set(), set()

    def weights_in(s):
        if s not in waited:
            waited.add(s)
            with scope(f"w{s}"):
                loaded(("w", s), w.at[s])

    def turn(other, s, mats=(0, 1)):
        weights_in(s)
        turned.add((other, s))
        with scope(f"turn{other}{s}"):
            for m in mats:
                wt[s, other, m] = w[s, other, m].T

    def relay(s):
        landed(("zin", s), own.at[s, pl.ds(0, nz - 1), 0])
        for d in ring:
            piece = own.at[s, z_pair[d], y]
            send(("yin", s), piece, piece, y_peer)
        send(("cin", s), own.at[s, :, y], oth.at[s, :, y], core_peer)

    def share(s):
        landed(("yin", s), own.at[s, :, 0])
        send(("cin", s), own.at[s, :, 1 - y], oth.at[s, :, 1 - y], core_peer)

    started = []

    def forward(other, s, also=()):
        weights_in(s)
        if other == 1:
            landed(("cin", s), oth.at[s])
        for _, t in also:
            weights_in(t)
        turned.update(also)
        with scope(f"fwd{other}{s}"):
            block = (own if other == 0 else oth)[s].reshape(blocks * UNIT, width)
            for m in (0, 1):
                for o, t in also:
                    wt[t, o, m] = w[t, o, m].T
                term = jnp.dot(block, w[s, other, m], preferred_element_type=jnp.float32)
                if started:
                    acc[m] += term
                else:
                    acc[m] = term
            started.append(s)

    own_out(1)
    own_out(2)
    turn(0, 0)
    own_out(3)
    turn(1, 0)
    own_out(4)
    turn(0, 3)
    own_out(5)
    turn(1, 3)
    relay(0)
    turn(1, 1)
    relay(1)
    turn(0, 1)
    turn(1, 2)
    relay(2)
    turn(0, 2)
    relay(3)
    turn(1, 4, [0])
    relay(4)
    turn(1, 4, [1])
    share(0)
    relay(5)
    forward(0, 0)
    share(1)
    forward(0, 1)
    share(2)
    forward(0, 2)
    forward(1, 0)
    share(3)
    forward(1, 1)
    forward(0, 3)
    share(4)
    forward(1, 2)
    forward(0, 4)
    share(5)
    forward(1, 3)
    forward(1, 4)
    forward(0, 5)
    forward(1, 5)

    loaded(("dh",), dhv.at[0])
    landed(("dhin",), dhv.at[0])
    tile = 256 if half % 256 == 0 else half
    with scope("epilogue"):
        for n in range(0, half, tile):
            cols = slice(n, n + tile)
            gate_value, up_value = acc[0, :, cols], acc[1, :, cols]
            first = dhv[0, :, cols].astype(jnp.float32).reshape(blocks, UNIT // 2, tile)
            second = dhv[1, :, cols].astype(jnp.float32).reshape(blocks, UNIT // 2, tile)
            upstream = jnp.stack([first, second], axis=1).reshape(blocks * UNIT, tile)
            sigmoid_gate = jax.nn.sigmoid(gate_value)
            activated = gate_value * sigmoid_gate
            hidden = (activated * up_value).reshape(blocks, 2, UNIT // 2, tile)
            for q in (0, 1):
                hst[q, :, cols] = hidden[:, q].reshape(blocks * UNIT // 2, tile).astype(jnp.bfloat16)
            dgv[:, cols] = (
                upstream * up_value * sigmoid_gate * (1.0 + gate_value * (1.0 - sigmoid_gate))
            ).astype(jnp.bfloat16)
            duv[:, cols] = (upstream * activated).astype(jnp.bfloat16)
    load(("hid",), hst.at[c], hid.at[:, mine])

    def backward(other, s):
        if (other, s) in turned:
            return jnp.dot(
                dgv[...], wt[s, other, 0], preferred_element_type=jnp.float32
            ) + jnp.dot(duv[...], wt[s, other, 1], preferred_element_type=jnp.float32)
        contract = (((1,), (1,)), ((), ()))
        return lax.dot_general(
            dgv[...], w[s, other, 0], contract, preferred_element_type=jnp.float32
        ) + lax.dot_general(duv[...], w[s, other, 1], contract, preferred_element_type=jnp.float32)

    turn_of = {}

    def back_other(s):
        turn_of[s] = len(turn_of) % 2
        with scope(f"bwd1{s}"):
            csend[s] = backward(1, s).reshape(nz, ny, UNIT, width).astype(jnp.bfloat16)
        for n in (1 - y, y):
            send(("csum", s, n is y), csend.at[s, :, n], crecv.at[s, :, n], core_peer)

    def back_own(s):
        with scope(f"bwd0{s}"):
            full[turn_of[s]] = backward(0, s).reshape(nz, ny, UNIT, width)

    def core_sum(s, where):
        return full[turn_of[s], where[0], where[1]] + crecv[s, where[0], where[1]].astype(jnp.float32)

    def core_add(s):
        landed(("csum", s, False), crecv.at[s, :, 0])
        if s == lead:
            landed(("csum", s, True), crecv.at[s, :, 0])
            for d in ring:
                for n in range(ny):
                    zsend_f[d - 1, n] = core_sum(s, (z_pair[d], n)).astype(jnp.bfloat16)
                send(("zsum", s), zsend_f.at[d - 1], zrecv_f.at[z_slot[d]], z_peer[d])
            for n in range(ny):
                keep_f[n] = core_sum(s, (z, n))
        else:
            for d in [*ring, 0]:
                ysend[s, d] = core_sum(s, (z_pair[d] if d else z, 1 - y)).astype(jnp.bfloat16)
                send(("ysum", s, d), ysend.at[s, d], yrecv.at[s, d], y_peer)
            landed(("csum", s, True), crecv.at[s, :, 0])
            for d in [*ring, 0]:
                keep[s, d] = core_sum(s, (z_pair[d] if d else z, y))

    def lead_add():
        landed(("zsum", lead), zrecv_f)
        total = keep_f[...]
        for d in ring:
            total = total + zrecv_f[d - 1].astype(jnp.float32)
        keep_f[...] = total
        ysend_f[...] = keep_f[1 - y].astype(jnp.bfloat16)
        send(("ysum", lead), ysend_f, yrecv_f, y_peer)

    def y_sum(s, d):
        landed(("ysum", s, d), yrecv.at[s, d])
        return keep[s, d] + yrecv[s, d].astype(jnp.float32)

    def y_add(s):
        for d in ring:
            zsend[s, d - 1] = y_sum(s, d).astype(jnp.bfloat16)
            send(("zsum", s), zsend.at[s, d - 1], zrecv.at[s, z_slot[d]],
                 (xz_peer if s < half_steps else z_peer)[d])

    def hand_over(s):
        xsend[s] = y_sum(s, 0)
        send(("xsum", s), xsend.at[s], xrecv.at[s], x_peer)

    def finish(s):
        if s == lead:
            landed(("ysum", s), yrecv_f)
            done = keep_f[y] + yrecv_f[...].astype(jnp.float32)
        else:
            if s < half_steps:
                landed(("xsum", s), xrecv.at[s])
                done = xrecv[s]
            else:
                done = y_sum(s, 0)
            landed(("zsum", s), zrecv.at[s])
            for d in ring:
                done = done + zrecv[s, d - 1].astype(jnp.float32)
        cols = slice((s % half_steps) * width, (s % half_steps + 1) * width)
        slots[1 - x if s < half_steps else x, :, cols] = done

    back_other(0)
    back_own(0)
    back_other(3)
    core_add(0)
    send(("hidin",), hst.at[1 - c], hid.at[:, mine], core_peer)
    back_own(3)
    back_other(1)
    core_add(3)
    back_own(1)
    back_other(2)
    core_add(1)
    back_own(2)
    back_other(4)
    core_add(2)
    y_add(0)
    hand_over(0)
    back_own(4)
    back_other(5)
    core_add(4)
    back_own(5)
    y_add(1)
    hand_over(1)
    core_add(5)
    y_add(2)
    hand_over(2)
    y_add(4)
    lead_add()
    y_add(5)
    finish(0)
    finish(1)
    finish(2)
    finish(3)
    finish(4)
    finish(5)

    loaded(("hid",), hst.at[0])
    landed(("hidin",), hst.at[0])
    with scope("sent"):
        every = w.reshape(2 * CORES * STEPS * width, half)
        rows_sent = sent_bytes[0] // (half * w.dtype.itemsize)
        pltpu.make_async_copy(every.at[pl.ds(0, rows_sent)], every.at[pl.ds(0, rows_sent)], send_sem.at[0]).wait()


def fused_body(nz, ny, tokens, expert_ids, gate_weight, up_weight, d_hidden):
    count, features = tokens.shape
    hidden_units = gate_weight.shape[1]
    rows = d_hidden.shape[0]
    width = features // (CORES * STEPS)
    half = hidden_units // CORES
    blocks = nz * ny
    half_steps = STEPS // 2
    bf, f32 = jnp.bfloat16, jnp.float32
    loads = STEPS * 2 + 2
    recvs = STEPS * 5 + (STEPS - 1) * (nz - 1) + STEPS // 2 + 2
    hbm = pl.BlockSpec(memory_space=pl.ANY)
    vmem = pl.BlockSpec(memory_space=pltpu.VMEM)
    flops = 8 * blocks * UNIT * features * half
    ids = expert_ids.T
    staged, slots, placed = pl.pallas_call(
        functools.partial(expert_kernel, nz, ny),
        out_shape=(
            pltpu.VMEM((rows, hidden_units), bf),
            pltpu.VMEM((CORES, UNIT, half_steps * width), f32),
            pltpu.VMEM((count, CORES * UNIT), f32),
        ),
        in_specs=[hbm, vmem, hbm, hbm, hbm],
        out_specs=(vmem, vmem, vmem),
        scratch_shapes=[
            pltpu.VMEM((STEPS, count, width), bf),
            pltpu.VMEM((STEPS, nz, ny, UNIT, width), bf),
            pltpu.VMEM((STEPS, nz, ny, UNIT, width), bf),
            pltpu.VMEM((STEPS, 2, 2, width, half), bf),
            pltpu.VMEM((STEPS, 2, 2, half, width), bf),
            pltpu.VMEM((2, blocks * UNIT, half), f32),
            pltpu.VMEM((2, rows, half), bf),
            pltpu.VMEM((blocks * UNIT, half), bf),
            pltpu.VMEM((blocks * UNIT, half), bf),
            pltpu.VMEM((2, rows, half), bf),
            pltpu.VMEM((STEPS, nz, ny, UNIT, width), bf),
            pltpu.VMEM((STEPS, nz, ny, UNIT, width), bf),
            pltpu.VMEM((2, nz, ny, UNIT, width), f32),
            pltpu.VMEM((STEPS, nz, UNIT, width), f32),
            pltpu.VMEM((STEPS, nz, UNIT, width), bf),
            pltpu.VMEM((STEPS, nz, UNIT, width), bf),
            pltpu.VMEM((STEPS, nz - 1, UNIT, width), bf),
            pltpu.VMEM((STEPS, nz - 1, UNIT, width), bf),
            pltpu.VMEM((half_steps, UNIT, width), f32),
            pltpu.VMEM((half_steps, UNIT, width), f32),
            pltpu.VMEM((nz - 1, ny, UNIT, width), bf),
            pltpu.VMEM((nz - 1, ny, UNIT, width), bf),
            pltpu.VMEM((ny, UNIT, width), f32),
            pltpu.VMEM((UNIT, width), bf),
            pltpu.VMEM((UNIT, width), bf),
            pltpu.SemaphoreType.DMA((loads,)),
            pltpu.SemaphoreType.DMA((1,)),
            pltpu.SemaphoreType.DMA((recvs,)),
        ],
        compiler_params=pltpu.CompilerParams(
            collective_id=0, has_side_effects=True, vmem_limit_bytes=62 * 1024 * 1024),
        cost_estimate=pl.CostEstimate(
            flops=flops, bytes_accessed=4 * features * half, transcendentals=0),
    )(tokens, ids, gate_weight, up_weight, d_hidden)
    d_tokens, hidden = pl.pallas_call(
        place_kernel,
        out_shape=(
            jax.ShapeDtypeStruct((count, half_steps * width), f32),
            jax.ShapeDtypeStruct((rows, hidden_units), bf),
        ),
        in_specs=[vmem, vmem, vmem],
        out_specs=(hbm, hbm),
        scratch_shapes=[
            pltpu.VMEM((half_steps, count, width), f32),
            pltpu.SemaphoreType.DMA((half_steps + 1,)),
        ],
    )(*[pltpu.with_memory_space_constraint(v, pltpu.VMEM) for v in (placed, slots, staged)])
    return hidden, d_tokens


def split_of(mesh):
    line = mesh.devices.reshape(mesh.shape["pipe"], mesh.shape["expert"])[0]
    coords = [getattr(device, "coords", None) for device in line]
    if coords[0] is None:
        return len(line) // 2, 2
    ny = len({tuple(at)[1] for at in coords})
    return len(line) // ny, ny


def solution(mesh):
    in_specs = (
        P("expert", None),
        P("expert", None),
        P(None, "expert"),
        P(None, "expert"),
        P("pipe", "expert"),
    )
    out_specs = (P("pipe", "expert"), P("expert", "pipe"))
    nz, ny = split_of(mesh)
    fits = ny == 2 and nz in (2, 4) and mesh.shape["pipe"] == 2 * CORES and 2 * UNIT == CAP
    body = functools.partial(fused_body, nz, ny) if fits else plain_body
    return jax.shard_map(body, mesh=mesh, in_specs=in_specs, out_specs=out_specs, check_vma=False)
```
